128 devices in a mesh: node: 4 (over z), wide: 32 (over y, x, core).
Axes of the slice: x: 4, y: 4, z: 4, core: 2. Of those that a mesh axis runs over, the one named last changes fastest.
Arguments:
- tokens: bfloat16 [65536, 768], P(('node', 'wide')), may hold values from -6 to 6
- expert_index: int32 [65536, 1], P(('node', 'wide')), may hold values from 0 to 255; in each aligned block of 512 rows (0 to 511, 512 to 1023, ...) at most 4 rows name the same one
- norm_gain: float32 [768], replicated, may hold values from 0.5 to 1.5
- router_weight: float32 [768, 256], replicated, may hold values from -0.21875 to 0.21875
- expert_in: bfloat16 [256, 768, 3072], P(('node', 'wide')), may hold values from -0.21875 to 0.21875
- expert_out: bfloat16 [256, 3072, 768], P(('node', 'wide')), may hold values from -0.109375 to 0.109375
- post_gain: float32 [768], replicated, may hold values from 0.5 to 1.5
- dense_in: bfloat16 [3072, 768], P('node'), may hold values from -0.21875 to 0.21875
- scale_in: float32 [3072], P('node'), may hold values from 0.5 to 2
- dense_out: bfloat16 [3072, 768], P('node'), may hold values from -0.109375 to 0.109375
- scale_out: float32 [768], replicated, may hold values from 0.5 to 2
Outputs:
- layer_out: bfloat16 [65536, 768], P(('node', 'wide'))
The draws below stay inside these ranges and needn't reach their ends.
Inputs may be any that keep to these rules, and one draw needn't show every extreme that they name: `expert_index`: in each aligned block of 512 rows (the tokens of one device) no expert is named by more than 4 rows, a bound that some block reaches.
All inputs are finite; a program needn't handle non-finite values.
Results may differ from the reference program's by a relative error of at most 0.01.
Values may be sent and summed in bfloat16 or wider, within the bound.
No kernel may reach another device: no remote copies, remote signals or barrier semaphores. Data moves between devices by JAX's collectives and lax.ppermute only.
A program may use at most 128 MiB of HBM per device.

```python
import math
import jax
import jax.numpy as jnp
import numpy as np
from jax import lax

D = 768
FF = 3072
TOK_DEV = 512
EXPERTS = 256
CAP = 4
TOKENS = 65536
DEVICES = 128


def shard_levels(rng, extent, cuts, low, top_value):
    def one(dim, blocks):
        heights = jax.random.uniform(jax.random.fold_in(jax.random.fold_in(rng, 6), dim), (blocks,), jnp.float32, low / len(cuts), top_value / len(cuts))
        return jnp.repeat(jnp.exp(heights), extent[dim] // blocks).reshape((-1,) + (1,) * (len(extent) - dim - 1))

    loudness = one(*cuts[0])
    for cut in cuts[1:]:
        loudness = loudness * one(*cut)
    return loudness


def shared_out(stream_key, own, number, rows, number_of, top, most, skew):
    sequence = jax.random.permutation(stream_key, number_of)
    heavy_load, usual = portions_of(number_of, rows * top, most, skew, True), portions_of(number_of, rows * top, most, skew, False)
    places = jnp.arange(number_of)

    def named(tallies, turn):
        used = int((tallies > 0).sum())
        fixed = max(1, used // 4)
        moved = fixed + (places - fixed + turn * (used - fixed)) % max(1, number_of - fixed)
        return jnp.zeros((number_of,), jnp.int32).at[sequence[jnp.where(places < fixed, places, moved)]].set(jnp.asarray(tallies, jnp.int32))

    tallies = jnp.where(number % 4 == 0, named(heavy_load, number // 4), named(usual, number - number // 4 - 1))
    mixed = jax.random.permutation(jax.random.fold_in(own, 3), number_of)
    donor, receiver = mixed[0:number_of // 2 * 2:2], mixed[1:number_of // 2 * 2:2]
    slack = jnp.minimum(tallies[donor] - 1, most - tallies[receiver]) // 2
    slack = jnp.where((donor == sequence[0]) | (receiver == sequence[0]) | (tallies[receiver] == 0), 0, jnp.maximum(slack, 0))
    moved = jax.random.randint(jax.random.fold_in(own, 4), (number_of // 2,), 0, 1 << 20) % (slack + 1)
    tallies = tallies.at[donor].add(-moved).at[receiver].add(moved)
    labels = jnp.searchsorted(jnp.cumsum(tallies), jnp.arange(rows * top), side="right").astype(jnp.int32)
    table = labels.reshape(top, rows).T
    table = table[jax.random.permutation(jax.random.fold_in(own, 1), rows)]
    turn = jax.random.randint(jax.random.fold_in(own, 2), (rows, 1), 0, top)
    return jnp.take_along_axis(table, (jnp.arange(top)[None, :] + turn) % top, axis=1)


def portions_of(number_of, total, limit, lean, full):
    loads = [(1 << 20) // math.isqrt(grade ** lean) + 1 for grade in range(1, number_of + 1)]
    largest = limit if full else min(limit, max(-(-total // number_of), total * loads[0] // sum(loads)))
    least = 1 if total - largest >= number_of - 1 else 0
    holding, spare = [largest] + [least] * (number_of - 1), total - largest - least * (number_of - 1)
    while spare > 0:
        free = [i for i in range(1, number_of) if holding[i] < largest] or [i for i in range(1, number_of) if holding[i] < limit]
        mass, budget = sum([loads[i] for i in free]), spare
        for i in free:
            more = min(limit - holding[i], max(1, budget * loads[i] // mass), spare)
            holding[i] = holding[i] + more
            spare = spare - more
    return np.array(holding)


def centred(own_key, shape, width, reach, pieces=(), kind=jnp.bfloat16):
    drawn = jax.random.normal(own_key, shape, jnp.float32) * width
    if len(pieces) > 0:
        drawn = shard_levels(own_key, shape, pieces, -0.22, 0.18) * drawn
    return jnp.clip(drawn, min=-reach, max=reach).astype(kind)


def setup_inputs(seed: int = 0) -> dict:
    arg_keys = jax.random.split(jax.random.key(seed), 12)
    tokens = centred(arg_keys[0], (TOKENS, D), 1.0, 6.0, ((0, 128),))
    expert_index_keys = jax.random.split(jax.random.fold_in(arg_keys[1], 1), TOKENS // TOK_DEV)
    expert_index_turns = jax.random.permutation(jax.random.fold_in(arg_keys[1], 3), TOKENS // TOK_DEV)
    expert_index = jax.vmap(lambda own, number: shared_out(jax.random.fold_in(arg_keys[1], 2), own, number, TOK_DEV, EXPERTS, 1, CAP, 2))(expert_index_keys, expert_index_turns).reshape((TOKENS, 1))
    norm_gain = jnp.clip(1.0 + 0.1 * jax.random.normal(arg_keys[2], (D,), jnp.float32), 0.5, 1.5)
    router_weight = centred(arg_keys[3], (D, EXPERTS), D ** -0.5, 0.21875, (), jnp.float32)
    expert_in = centred(arg_keys[4], (EXPERTS, D, FF), D ** -0.5, 0.21875, ((0, 128),))
    expert_out = centred(arg_keys[5], (EXPERTS, FF, D), FF ** -0.5, 0.109375, ((0, 128),))
    post_gain = jnp.clip(1.0 + 0.1 * jax.random.normal(arg_keys[6], (D,), jnp.float32), 0.5, 1.5)
    dense_in = centred(arg_keys[7], (FF, D), D ** -0.5, 0.21875, ((0, 4),))
    scale_in = jnp.clip(jnp.exp(math.log(2.0) - 1.3862944 * jax.random.uniform(arg_keys[8], (FF,), jnp.float32) ** shard_levels(arg_keys[8], (FF,), ((0, 4),), -0.2, 0.2)), 0.5, 2.0)
    dense_out = centred(arg_keys[9], (FF, D), FF ** -0.5, 0.109375, ((0, 4),))
    scale_out = jnp.clip(jnp.exp(jax.random.uniform(arg_keys[10], (D,), jnp.float32, math.log(0.5), math.log(2.0))), 0.5, 2.0)
    return dict(tokens=tokens, expert_index=expert_index, norm_gain=norm_gain, router_weight=router_weight, expert_in=expert_in, expert_out=expert_out, post_gain=post_gain, dense_in=dense_in, scale_in=scale_in, dense_out=dense_out, scale_out=scale_out)


def root_norm(values, gain_vector):
    floats = values.astype(jnp.float32)
    square_mean = lax.optimization_barrier(jnp.mean(floats * floats, axis=-1, keepdims=True))
    return (floats * lax.rsqrt(square_mean + 1e-06) * gain_vector).astype(jnp.bfloat16)

def reference(tokens, expert_index, norm_gain, router_weight, expert_in, expert_out, post_gain, dense_in, scale_in, dense_out, scale_out):
    normed = root_norm(tokens, norm_gain)
    chosen = expert_index[:, 0].astype(jnp.int32)
    logits = jnp.dot(normed.astype(jnp.float32), router_weight, precision=lax.Precision.HIGHEST)
    picked_logit = jnp.take_along_axis(logits, chosen[:, None], axis=1)[:, 0]
    gate_prob = 1.0 / (1.0 + jnp.exp(-picked_logit))
    expert_room = DEVICES * CAP
    counts = jnp.zeros((EXPERTS,), jnp.int32).at[chosen].add(1)
    starts = (jnp.cumsum(counts) - counts).astype(jnp.int32)
    sorted_order = jnp.argsort(chosen, stable=True).astype(jnp.int32)
    placement_index = jnp.zeros((TOKENS,), jnp.int32).at[sorted_order].set(jnp.arange(TOKENS, dtype=jnp.int32))
    expert_rank = (placement_index - starts[chosen]).astype(jnp.int32)
    ordered = jnp.concatenate([normed[sorted_order], jnp.zeros((expert_room, D), jnp.bfloat16)], axis=0)

    def one_expert(expert):
        expert_rows = lax.dynamic_slice_in_dim(ordered, starts[expert], expert_room, 0)
        hidden = jax.nn.relu(jnp.dot(expert_rows, expert_in[expert], preferred_element_type=jnp.float32)).astype(jnp.bfloat16)
        return jnp.dot(hidden, expert_out[expert], preferred_element_type=jnp.float32).astype(jnp.bfloat16)
    results = lax.map(one_expert, jnp.arange(EXPERTS, dtype=jnp.int32))
    flat_index = (chosen * expert_room + expert_rank).astype(jnp.int32)
    expert_result = results.reshape(EXPERTS * expert_room, D)[flat_index]
    residual = (tokens.astype(jnp.float32) + gate_prob[:, None] * expert_result.astype(jnp.float32)).astype(jnp.bfloat16)
    normed2 = root_norm(residual, post_gain)
    projected = lax.dot_general(normed2, dense_in, (((1,), (1,)), ((), ())), preferred_element_type=jnp.float32)
    hidden = jax.nn.relu(projected * scale_in[None, :]).astype(jnp.bfloat16)
    dense_sum = jnp.dot(hidden, dense_out, preferred_element_type=jnp.float32)
    return (residual.astype(jnp.float32) + dense_sum * scale_out[None, :]).astype(jnp.bfloat16)
```

```python
import functools

import jax
import jax.numpy as jnp
from jax import lax
from jax.experimental import pallas as pl
from jax.experimental.pallas import tpu as pltpu
from jax.sharding import PartitionSpec as P

AXES = ("node", "wide")
Y_CHIPS, X_CHIPS, CORES = 4, 4, 2
LANES = 128
SUB = 8
BF16 = jnp.bfloat16
F32 = jnp.float32


def moved(value, nodes, dz=0, dy=0, dx=0, dc=0):
    def place(z, y, x, c):
        return ((z * Y_CHIPS + y) * X_CHIPS + x) * CORES + c

    pairs = [
        (
            place(z, y, x, c),
            place((z + dz) % nodes, (y + dy) % Y_CHIPS, (x + dx) % X_CHIPS, (c + dc) % CORES),
        )
        for z in range(nodes)
        for y in range(Y_CHIPS)
        for x in range(X_CHIPS)
        for c in range(CORES)
    ]
    return lax.ppermute(value, AXES, pairs)


def joined(first, second):
    top = lax.broadcasted_iota(jnp.int32, first.shape, 1) < SUB // 2
    even = jnp.where(top, first, pltpu.roll(second, SUB // 2, 1))
    odd = jnp.where(top, pltpu.roll(first, SUB // 2, 1), second)
    return even, odd


def pack_columns(rows, block, out_ref):
    count = rows.shape[0] // SUB
    first = rows[:, :LANES].reshape(count, SUB, LANES)
    second = rows[:, LANES:].reshape(count, SUB, LANES)
    even, odd = joined(first, second)
    out_ref[:, 0, pl.ds(block * SUB, SUB), :] = even.astype(out_ref.dtype)
    out_ref[:, 1, pl.ds(block * SUB, SUB), :] = odd.astype(out_ref.dtype)


def unpack_messages(message_ref, rows_ref):
    count = message_ref.shape[0]
    for block in range(message_ref.shape[2] // SUB):
        even = message_ref[:, 0, block * SUB : (block + 1) * SUB, :].astype(F32)
        odd = message_ref[:, 1, block * SUB : (block + 1) * SUB, :].astype(F32)
        first, second = joined(even, odd)
        start = block * 2 * LANES
        rows_ref[:, start : start + LANES] = first.reshape(count * SUB, LANES).astype(BF16)
        rows_ref[:, start + LANES : start + 2 * LANES] = second.reshape(count * SUB, LANES).astype(BF16)


def dispatch_kernel(capacity, token_ref, column_ref, row_ref, gain_ref, zero_ref, one_ref):
    floats = token_ref[...].astype(F32)
    square_mean = jnp.mean(floats * floats, axis=-1, keepdims=True)
    normed = (floats * lax.rsqrt(square_mean + 1e-06) * gain_ref[...]).astype(BF16)
    count = floats.shape[0]
    row = row_ref[...]
    source = lax.broadcasted_iota(jnp.int32, (count, count), 0)
    target = lax.broadcasted_iota(jnp.int32, (count, count), 1)
    same = (column_ref[...] == row) & (source < target)
    slot = jnp.sum(jnp.where(same, 1, 0), axis=0, keepdims=True)
    place = (row >> 1) * capacity + slot
    for held, out_ref in enumerate((zero_ref, one_ref)):
        position = jnp.where((row & 1) == held, place, -1)
        selected = jnp.where(source == position, 1.0, 0.0).astype(BF16)
        for block in range(3):
            columns = normed[:, block * 2 * LANES : (block + 1) * 2 * LANES]
            rows = jnp.dot(selected, columns, preferred_element_type=F32)
            pack_columns(rows, block, out_ref)


def expert_kernel(held, message_ref, in_hbm, out_hbm, result_ref, rows, hidden, w_in, w_out, sems):
    in_tile, out_tile = 512, 256
    in_steps, out_steps = hidden.shape[1] // in_tile, rows.shape[1] // out_tile

    def in_copy(step):
        columns = pl.ds(step * in_tile, in_tile)
        return pltpu.make_async_copy(in_hbm.at[held, :, columns], w_in.at[:, columns], sems.at[step])

    def out_copy(step):
        columns = pl.ds(step * out_tile, out_tile)
        return pltpu.make_async_copy(
            out_hbm.at[held, :, columns], w_out.at[:, columns], sems.at[in_steps + step]
        )

    for step in range(in_steps):
        in_copy(step).start()
    for step in range(out_steps):
        out_copy(step).start()
    unpack_messages(message_ref, rows)

    for step in range(in_steps):
        in_copy(step).wait()
        columns = slice(step * in_tile, (step + 1) * in_tile)
        value = jnp.dot(rows[...], w_in[:, columns], preferred_element_type=F32)
        hidden[:, columns] = jnp.maximum(value, 0.0).astype(BF16)
    for step in range(out_steps):
        out_copy(step).wait()
        columns = slice(step * out_tile, (step + 1) * out_tile)
        value = jnp.dot(hidden[...], w_out[:, columns], preferred_element_type=F32)
        pack_columns(value, step, result_ref)


def tail_kernel(
    pieces,
    token_ref,
    gate_ref,
    place_ref,
    gain_ref,
    scale_ref,
    scale_out_ref,
    far_scale_ref,
    zero_ref,
    one_ref,
    own_in,
    own_out,
    *rest,
):
    arrays, (result_ref, w_in, w_out, rows, normed2, hidden, total, sems) = rest[:-8], rest[-8:]
    width = token_ref.shape[1]
    shard = own_in.shape[0]
    wide = lax.axis_index("wide")
    at = {"x": (wide // CORES) % X_CHIPS, "y": wide // (CORES * X_CHIPS), "c": wide % CORES}
    copies = [
        pltpu.make_async_copy(own_in, w_in.at[pl.ds(0, shard), :], sems.at[0]),
        pltpu.make_async_copy(own_out, w_out.at[pl.ds(0, shard), :], sems.at[1]),
    ]
    for index, (axis, half, offset, swapped) in enumerate(pieces):
        array = arrays[index]
        size = array.shape[0] // 6
        line = (at[axis] + offset) % 4
        core = (at["c"] + swapped) % CORES
        first = half * (shard // 2) + (line * CORES + core) * size
        for far in range(3):
            start = pl.multiple_of(shard * (far + 1) + first, 16)
            for which, weights in enumerate((w_in, w_out)):
                copies.append(
                    pltpu.make_async_copy(
                        array.at[pl.ds((far * 2 + which) * size, size), :],
                        weights.at[pl.ds(start, size), :],
                        sems.at[2 + index],
                    )
                )
    for copy in copies:
        copy.start()

    count = token_ref.shape[0]
    slots = lax.broadcasted_iota(jnp.int32, (count, count), 1)
    for held, message_ref in enumerate((zero_ref, one_ref)):
        unpack_messages(message_ref, rows)
        picked = jnp.where(slots == place_ref[:, held : held + 1], 1.0, 0.0).astype(BF16)
        value = jnp.dot(picked, rows[...], preferred_element_type=F32)
        total[...] = value if held == 0 else total[...] + value
    residual = (token_ref[...].astype(F32) + gate_ref[...] * total[...]).astype(BF16)
    rows[...] = residual
    floats = residual.astype(F32)
    square_mean = jnp.mean(floats * floats, axis=-1, keepdims=True)
    normed2[...] = (floats * lax.rsqrt(square_mean + 1e-06) * gain_ref[...]).astype(BF16)

    tile = 256
    steps = shard // tile

    def columns_of(block, scale):
        for step in range(steps):
            start = pl.multiple_of(block * shard + step * tile, tile)
            value = lax.dot_general(
                normed2[...],
                w_in[pl.ds(start, tile), :],
                (((1,), (1,)), ((), ())),
                preferred_element_type=F32,
            )
            value = jnp.maximum(value * scale[:, step * tile : (step + 1) * tile], 0.0)
            hidden[:, pl.ds(start, tile)] = value.astype(BF16)

    copies[0].wait()
    columns_of(0, scale_ref[...])
    for copy in copies[1:]:
        copy.wait()

    def far_block(block, carry):
        columns_of(block, far_scale_ref[block - 1])
        return carry

    lax.fori_loop(1, 4, far_block, 0)
    for step in range(width // tile):
        columns = slice(step * tile, (step + 1) * tile)
        value = jnp.dot(hidden[...], w_out[:, columns], preferred_element_type=F32)
        value = rows[:, columns].astype(F32) + value * scale_out_ref[:, columns]
        result_ref[:, columns] = value.astype(BF16)


def vmem():
    return pl.BlockSpec(memory_space=pltpu.VMEM)


def anywhere():
    return pl.BlockSpec(memory_space=pl.ANY)


def cost(flops, moved_bytes):
    return pl.CostEstimate(flops=int(flops), bytes_accessed=int(moved_bytes), transcendentals=0)


def per_device(
    tokens,
    expert_index,
    norm_gain,
    router_weight,
    expert_in,
    expert_out,
    post_gain,
    dense_in,
    scale_in,
    dense_out,
    scale_out,
):
    tok_dev, width = tokens.shape
    experts = router_weight.shape[1]
    held_experts, _, hidden_units = expert_in.shape
    devices = experts // held_experts
    capacity = max(2, 2 * tok_dev // experts)
    shard = dense_in.shape[0]
    nodes = hidden_units // shard
    wide = lax.axis_index("wide")
    core, x_chip, y_chip = wide % CORES, (wide // CORES) % X_CHIPS, wide // (CORES * X_CHIPS)
    message = (devices // 2, 2, capacity * width // LANES, LANES)
    shapes = [jax.ShapeDtypeStruct(message, BF16)] * 2

    sent = pl.pallas_call(
        functools.partial(dispatch_kernel, capacity),
        out_shape=shapes,
        in_specs=[vmem()] * 4,
        out_specs=[vmem()] * 2,
        cost_estimate=cost(4 * tok_dev * tok_dev * width, 4e6),
        name="dispatch",
    )(tokens, expert_index, expert_index.reshape(1, tok_dev), norm_gain.reshape(1, width))

    def exchanged(value):
        flat = value.reshape((devices,) + message[2:])
        return lax.all_to_all(flat, AXES, split_axis=0, concat_axis=0, tiled=True).reshape(message)

    arrived = [exchanged(value) for value in sent]

    size = shard // 2 // (X_CHIPS * CORES)
    a_start = (x_chip * CORES + core) * size
    b_start = shard // 2 + (y_chip * CORES + core) * size
    high = lax.reduce_precision(scale_in, 8, 7)
    middle = lax.reduce_precision(scale_in - high, 8, 7)
    low = scale_in - high - middle
    blank = jnp.zeros_like(scale_in)
    scale_rows = jnp.stack([high, middle, low] + [blank] * 5).astype(BF16)
    own = jnp.concatenate(
        [
            lax.dynamic_slice_in_dim(codes, start, size, 0)
            for start in (a_start, b_start)
            for codes in (dense_in, dense_out)
        ]
        + [scale_rows],
        axis=0,
    )
    far = [moved(own, nodes, dz=step) for step in (1, -1, 2)]
    along = {
        "x": jnp.concatenate([value[: 2 * size] for value in far], axis=0),
        "y": jnp.concatenate([value[2 * size : 4 * size] for value in far], axis=0),
    }
    far_scales = jnp.stack(
        [value[4 * size : 4 * size + 3].astype(F32).sum(axis=0, keepdims=True) for value in far]
    )
    pieces, arrays = [], []
    for half, axis in enumerate(("x", "y")):
        for offset, step in ((0, 0), (-1, 1), (1, -1), (2, 2)):
            value = along[axis]
            if step:
                value = moved(value, nodes, **{"d" + axis: step})
            pieces.append((axis, half, offset % 4, 0))
            arrays.append(value)
            pieces.append((axis, half, offset % 4, 1))
            arrays.append(moved(value, nodes, dc=1))

    floats = tokens.astype(F32)
    square_mean = jnp.mean(floats * floats, axis=-1, keepdims=True)
    normed = (floats * lax.rsqrt(square_mean + 1e-06) * norm_gain).astype(BF16)
    chosen = expert_index[:, 0]
    columns = lax.broadcasted_iota(jnp.int32, (tok_dev, experts), 1)
    picked = chosen[:, None] == columns
    logits = jnp.dot(normed.astype(F32), router_weight, precision=lax.Precision.HIGHEST)
    picked_logit = jnp.sum(jnp.where(picked, logits, 0.0), axis=1)
    gate_prob = 1.0 / (1.0 + jnp.exp(-picked_logit))
    ranks = lax.broadcasted_iota(jnp.int32, (tok_dev, tok_dev), 0)
    others = lax.broadcasted_iota(jnp.int32, (tok_dev, tok_dev), 1)
    earlier = (chosen[:, None] == chosen[None, :]) & (others < ranks)
    slot = jnp.sum(earlier.astype(jnp.int32), axis=1)
    place = (chosen >> 1) * capacity + slot
    places = jnp.stack([jnp.where((chosen & 1) == held, place, -1) for held in range(2)], axis=1)

    returned = []
    for held in range(held_experts):
        in_steps, out_steps = hidden_units // 512, width // 256
        produced = pl.pallas_call(
            functools.partial(expert_kernel, held),
            out_shape=shapes[0],
            in_specs=[vmem(), anywhere(), anywhere()],
            out_specs=vmem(),
            scratch_shapes=[
                pltpu.VMEM((devices * capacity, width), BF16),
                pltpu.VMEM((devices * capacity, hidden_units), BF16),
                pltpu.VMEM((width, hidden_units), BF16),
                pltpu.VMEM((hidden_units, width), BF16),
                pltpu.SemaphoreType.DMA((in_steps + out_steps,)),
            ],
            compiler_params=pltpu.CompilerParams(vmem_limit_bytes=24 << 20),
            cost_estimate=cost(4 * tok_dev * hidden_units * width, 1.2e7),
            name=f"expert{held}",
        )(arrived[held], expert_in, expert_out)
        returned.append(exchanged(produced))

    return pl.pallas_call(
        functools.partial(tail_kernel, tuple(pieces)),
        out_shape=jax.ShapeDtypeStruct(tokens.shape, BF16),
        in_specs=[vmem()] * 9 + [anywhere()] * (2 + len(arrays)),
        out_specs=vmem(),
        scratch_shapes=[
            pltpu.VMEM((hidden_units, width), BF16),
            pltpu.VMEM((hidden_units, width), BF16),
            pltpu.VMEM((tok_dev, width), BF16),
            pltpu.VMEM((tok_dev, width), BF16),
            pltpu.VMEM((tok_dev, hidden_units), BF16),
            pltpu.VMEM((tok_dev, width), F32),
            pltpu.SemaphoreType.DMA((2 + len(arrays),)),
        ],
        compiler_params=pltpu.CompilerParams(vmem_limit_bytes=32 << 20),
        cost_estimate=cost(4 * tok_dev * hidden_units * width, 1.2e7),
        name="tail",
    )(
        tokens,
        gate_prob[:, None],
        places,
        post_gain.reshape(1, width),
        scale_in.reshape(1, shard),
        scale_out.reshape(1, width),
        far_scales,
        returned[0],
        returned[1],
        dense_in,
        dense_out,
        *arrays,
    )


def solution(mesh):
    return jax.shard_map(
        per_device,
        mesh=mesh,
        in_specs=(
            P(("node", "wide"), None),
            P(("node", "wide"), None),
            P(),
            P(),
            P(("node", "wide"), None, None),
            P(("node", "wide"), None, None),
            P(),
            P("node", None),
            P("node"),
            P("node", None),
            P(),
        ),
        out_specs=P(("node", "wide"), None),
        check_vma=False,
    )
```

```python
import functools

import jax
import jax.numpy as jnp
from jax import lax
from jax.experimental import pallas as pl
from jax.experimental.pallas import tpu as pltpu
from jax.sharding import PartitionSpec as P

AXES = ("node", "wide")
Y_CHIPS, X_CHIPS, CORES = 4, 4, 2
COLORS = 4
FAR = 3
SCALE_ROWS = 8
LANES = 128
SUB = 8
BF16 = jnp.bfloat16
F32 = jnp.float32


def moved(value, nodes, dz=0, dy=0, dx=0, dc=0):
    def place(z, y, x, c):
        return ((z * Y_CHIPS + y) * X_CHIPS + x) * CORES + c

    pairs = [
        (
            place(z, y, x, c),
            place((z + dz) % nodes, (y + dy) % Y_CHIPS, (x + dx) % X_CHIPS, (c + dc) % CORES),
        )
        for z in range(nodes)
        for y in range(Y_CHIPS)
        for x in range(X_CHIPS)
        for c in range(CORES)
    ]
    return lax.ppermute(value, AXES, pairs)


def position():
    wide = lax.axis_index("wide")
    core = wide % CORES
    x_chip = (wide // CORES) % X_CHIPS
    y_chip = wide // (CORES * X_CHIPS)
    return core, ((x_chip + 2 * y_chip) % COLORS, (2 * x_chip + y_chip) % COLORS)


def joined(first, second):
    top = lax.broadcasted_iota(jnp.int32, first.shape, 1) < SUB // 2
    even = jnp.where(top, first, pltpu.roll(second, SUB // 2, 1))
    odd = jnp.where(top, pltpu.roll(first, SUB // 2, 1), second)
    return even, odd


def pack_columns(rows, block, out_ref):
    count = rows.shape[0] // SUB
    first = rows[:, :LANES].reshape(count, SUB, LANES)
    second = rows[:, LANES:].reshape(count, SUB, LANES)
    even, odd = joined(first, second)
    out_ref[:, 0, block * SUB : (block + 1) * SUB, :] = even.astype(out_ref.dtype)
    out_ref[:, 1, block * SUB : (block + 1) * SUB, :] = odd.astype(out_ref.dtype)


def unpack_messages(message_ref, held, rows_ref):
    count = message_ref.shape[0]
    blocks = rows_ref.shape[1] // (2 * LANES)
    for block in range(blocks):
        tile = slice((held * blocks + block) * SUB, (held * blocks + block + 1) * SUB)
        even = message_ref[:, 0, tile, :].astype(F32)
        odd = message_ref[:, 1, tile, :].astype(F32)
        first, second = joined(even, odd)
        start = block * 2 * LANES
        rows_ref[:, start : start + LANES] = first.reshape(count * SUB, LANES).astype(BF16)
        rows_ref[:, start + LANES : start + 2 * LANES] = second.reshape(count * SUB, LANES).astype(BF16)


def both_ways(row):
    count = row.shape[1]
    floats = row.astype(F32)
    turned = jnp.broadcast_to(floats, (LANES, count)).T
    along_rows = jnp.concatenate([turned] * (count // LANES), axis=1)
    return jnp.broadcast_to(floats, (count, count)), along_rows


def normed_rows(floats, gain):
    square_mean = jnp.mean(floats * floats, axis=-1, keepdims=True)
    return (floats * lax.rsqrt(square_mean + 1e-06) * gain).astype(BF16)


def cut_kernel(size, in_hbm, out_hbm, scale_ref, cut_ref, sems):
    half = in_hbm.shape[0] // 2
    core, colors = position()
    copies = []
    for part in range(2):
        start = pl.multiple_of(part * half + (colors[part] * CORES + core) * size, 16)
        for which, codes in enumerate((in_hbm, out_hbm)):
            copies.append(
                pltpu.make_async_copy(
                    codes.at[pl.ds(start, size), :],
                    cut_ref.at[pl.ds((part * 2 + which) * size, size), :],
                    sems.at[part * 2 + which],
                )
            )
    for copy in copies:
        copy.start()
    scale = scale_ref[...].reshape(1, -1)
    high = scale.astype(BF16).astype(F32)
    middle = (scale - high).astype(BF16).astype(F32)
    low = scale - high - middle
    lines = lax.broadcasted_iota(jnp.int32, (SCALE_ROWS, scale.shape[1]), 0)
    terms = jnp.where(lines == 0, high, jnp.where(lines == 1, middle, jnp.where(lines == 2, low, 0.0)))
    cut_ref[4 * size :, :] = terms.astype(BF16)
    for copy in copies:
        copy.wait()


def relay_kernel(size, *refs):
    far, (own, right, left, up, down, scales_ref, sems) = refs[:FAR], refs[FAR:]
    copies = []

    def copy(source, start, out, target):
        copies.append(
            pltpu.make_async_copy(
                source.at[pl.ds(start, size), :],
                out.at[pl.ds(target * size, size), :],
                sems.at[len(copies)],
            )
        )

    for index, source in enumerate(far):
        for part in range(2):
            whole, shared = ((right, left), (up, down))[part], ((up, down), (right, left))[part]
            for which in range(2):
                start = (part * 2 + which) * size
                copy(source, start, own, (index * 2 + part) * 2 + which)
                for out in whole:
                    copy(source, start, out, index * 2 + which)
                copy(source, start, shared[which], 2 * FAR + index)
    for one in copies:
        one.start()
    for index, source in enumerate(far):
        terms = source[4 * size :, :].astype(F32)
        scales_ref[index] = terms[0:1] + terms[1:2] + terms[2:3]
    for one in copies:
        one.wait()


def weave_copies(size, own_in, own_out, arrays, w_in, w_out, sems):
    shard = own_in.shape[0]
    core, colors = position()
    weights = (w_in, w_out)
    copies = [[[] for _ in range(FAR + 1)] for _ in range(2)]
    for which, own in enumerate((own_in, own_out)):
        copies[which][0].append(
            pltpu.make_async_copy(own, weights[which].at[pl.ds(0, shard), :], sems.at[which, 0])
        )

    def copy(array, row, index, part, which, color, swapped):
        line = (colors[part] + color) % COLORS
        line = line * CORES + (core + swapped) % CORES
        start = pl.multiple_of(shard * (index + 1) + part * (shard // 2) + line * size, 16)
        copies[which][index + 1].append(
            pltpu.make_async_copy(
                arrays[array].at[pl.ds(row * size, size), :],
                weights[which].at[pl.ds(start, size), :],
                sems.at[which, index + 1],
            )
        )

    for swapped in range(CORES):
        base = swapped * 5
        for index in range(FAR):
            for which in range(2):
                for part in range(2):
                    copy(base, (index * 2 + part) * 2 + which, index, part, which, 0, swapped)
                for side in range(4):
                    part, color = side // 2, (-1, 1)[side % 2]
                    copy(base + 1 + side, index * 2 + which, index, part, which, color, swapped)
                    if which == side % 2:
                        copy(base + 1 + side, 2 * FAR + index, index, 1 - part, which, 2, swapped)
    return copies


def dispatch_kernel(capacity, token_ref, row_ref, gain_ref, out_ref):
    normed = normed_rows(token_ref[...].astype(F32), gain_ref[...].reshape(1, -1))
    count = token_ref.shape[0]
    row = row_ref[...]
    along, across = both_ways(row)
    source = lax.broadcasted_iota(jnp.int32, (count, count), 0)
    target = lax.broadcasted_iota(jnp.int32, (count, count), 1)
    same = jnp.where((along == across) & (source < target), 1.0, 0.0)
    slot = jnp.sum(same, axis=0, keepdims=True).astype(jnp.int32)
    place = (row >> 1) * capacity + slot
    blocks = normed.shape[1] // (2 * LANES)
    for held in range(2):
        wanted = jnp.where((row & 1) == held, place, -1)
        selected = jnp.where(source == wanted, 1.0, 0.0).astype(BF16)
        for block in range(blocks):
            columns = normed[:, block * 2 * LANES : (block + 1) * 2 * LANES]
            rows = jnp.dot(selected, columns, preferred_element_type=F32)
            pack_columns(rows, held * blocks + block, out_ref)


def side_kernel(capacity, token_ref, row_ref, gain_ref, router_ref, gate_ref, place_ref):
    normed = normed_rows(token_ref[...].astype(F32), gain_ref[...].reshape(1, -1)).astype(F32)
    count = token_ref.shape[0]
    along, across = both_ways(row_ref[...])
    logits = jnp.dot(normed, router_ref[...], precision=lax.Precision.HIGHEST, preferred_element_type=F32)
    experts = logits.shape[1]
    columns = lax.broadcasted_iota(jnp.int32, (count, experts), 1).astype(F32)
    picked = jnp.sum(jnp.where(across[:, :experts] == columns, logits, 0.0), axis=1, keepdims=True)
    gate_ref[...] = 1.0 / (1.0 + jnp.exp(-picked))
    rank = lax.broadcasted_iota(jnp.int32, (count, count), 0)
    other = lax.broadcasted_iota(jnp.int32, (count, count), 1)
    same = jnp.where((along == across) & (other < rank), 1.0, 0.0)
    slot = jnp.sum(same, axis=1, keepdims=True).astype(jnp.int32)
    chosen = across[:, :1].astype(jnp.int32)
    place = (chosen >> 1) * capacity + slot
    for held in range(2):
        place_ref[:, held : held + 1] = jnp.where((chosen & 1) == held, place, -1)


def expert_kernel(message_ref, in_hbm, out_hbm, result_ref, rows, hidden, w_in, w_out, sems):
    held_experts, width, units = in_hbm.shape
    tile, parts = 512, 4
    copies = []
    for held in range(held_experts):
        for codes, weights in ((in_hbm, w_in), (out_hbm, w_out)):
            depth = codes.shape[1] // parts
            for part in range(parts):
                lines = pl.ds(part * depth, depth)
                copies.append(
                    pltpu.make_async_copy(
                        codes.at[held, lines, :], weights.at[held, lines, :], sems.at[len(copies)]
                    )
                )
    for copy in copies:
        copy.start()
    blocks = width // (2 * LANES)
    for held in range(held_experts):
        unpack_messages(message_ref, held, rows)
        first = held * 2 * parts
        for copy in copies[first : first + parts]:
            copy.wait()
        for step in range(units // tile):
            columns = slice(step * tile, (step + 1) * tile)
            value = jnp.dot(rows[...], w_in[held, :, columns], preferred_element_type=F32)
            hidden[:, columns] = jnp.maximum(value, 0.0).astype(BF16)
        for copy in copies[first + parts : first + 2 * parts]:
            copy.wait()
        for block in range(blocks):
            columns = slice(block * 2 * LANES, (block + 1) * 2 * LANES)
            value = jnp.dot(hidden[...], w_out[held, :, columns], preferred_element_type=F32)
            pack_columns(value, held * blocks + block, result_ref)


def tail_kernel(
    size,
    token_ref,
    gate_ref,
    place_ref,
    gain_ref,
    scale_ref,
    scale_out_ref,
    far_scale_ref,
    message_ref,
    own_in,
    own_out,
    *refs,
):
    arrays, (result_ref, w_in, w_out, rows, normed2, hidden, total, sems) = refs[:-8], refs[-8:]
    copies = weave_copies(size, own_in, own_out, arrays, w_in, w_out, sems)
    for side in copies:
        for node in side:
            for copy in node:
                copy.start()
    count, width = token_ref.shape
    slots = lax.broadcasted_iota(jnp.int32, (count, count), 1)
    for held in range(2):
        unpack_messages(message_ref, held, rows)
        picked = jnp.where(slots == place_ref[:, held : held + 1], 1.0, 0.0).astype(BF16)
        value = jnp.dot(picked, rows[...], preferred_element_type=F32)
        total[...] = value if held == 0 else total[...] + value
    residual = (token_ref[...].astype(F32) + gate_ref[...] * total[...]).astype(BF16)
    rows[...] = residual
    normed2[...] = normed_rows(residual.astype(F32), gain_ref[...].reshape(1, -1))

    tile = 256
    units = hidden.shape[1]
    shard = own_in.shape[0]
    own_scale = scale_ref[...].reshape(1, -1)
    for step in range(units // tile):
        block, inner = divmod(step * tile, shard)
        if inner == 0:
            for copy in copies[0][block]:
                copy.wait()
        scale = own_scale if block == 0 else far_scale_ref[block - 1]
        value = lax.dot_general(
            normed2[...],
            w_in[step * tile : (step + 1) * tile, :],
            (((1,), (1,)), ((), ())),
            preferred_element_type=F32,
        )
        value = jnp.maximum(value * scale[:, inner : inner + tile], 0.0)
        hidden[:, step * tile : (step + 1) * tile] = value.astype(BF16)
    for node in copies[1]:
        for copy in node:
            copy.wait()
    scale_out = scale_out_ref[...].reshape(1, -1)
    for step in range(width // tile):
        columns = slice(step * tile, (step + 1) * tile)
        value = jnp.dot(hidden[...], w_out[:, columns], preferred_element_type=F32)
        value = rows[:, columns].astype(F32) + value * scale_out[:, columns]
        result_ref[:, columns] = value.astype(BF16)


def vmem():
    return pl.BlockSpec(memory_space=pltpu.VMEM)


def hbm():
    return pl.BlockSpec(memory_space=pltpu.HBM)


def call(kernel, out_shape, in_specs, scratch=(), grant=16, flops=0, moved_bytes=0):
    return pl.pallas_call(
        kernel,
        out_shape=out_shape,
        in_specs=in_specs,
        out_specs=jax.tree.map(lambda _: vmem(), out_shape),
        scratch_shapes=list(scratch),
        compiler_params=pltpu.CompilerParams(vmem_limit_bytes=grant << 20),
        cost_estimate=pl.CostEstimate(
            flops=int(flops), bytes_accessed=int(moved_bytes), transcendentals=0
        ),
    )


def per_device(
    tokens,
    expert_index,
    norm_gain,
    router_weight,
    expert_in,
    expert_out,
    post_gain,
    dense_in,
    scale_in,
    dense_out,
    scale_out,
):
    tok_dev, width = tokens.shape
    experts = router_weight.shape[1]
    held_experts, _, units = expert_in.shape
    devices = experts // held_experts
    capacity = max(2, 2 * tok_dev // experts)
    shard = dense_in.shape[0]
    nodes = units // shard
    size = shard // 2 // (COLORS * CORES)
    message = (devices // 2, 2, held_experts * capacity * width // LANES, LANES)
    like = jax.ShapeDtypeStruct

    row = expert_index.reshape(1, tok_dev)
    dma = pltpu.SemaphoreType.DMA

    cut = call(
        functools.partial(cut_kernel, size),
        like((4 * size + SCALE_ROWS, width), BF16),
        [hbm(), hbm(), vmem()],
        [dma((4,))],
        grant=60,
        moved_bytes=6e5,
    )(dense_in, dense_out, scale_in)
    far = []
    for step in (1, -1, 2):
        far.append(moved(cut, nodes, dz=step))

    sent = call(
        functools.partial(dispatch_kernel, capacity),
        like(message, BF16),
        [vmem()] * 3,
        flops=4 * tok_dev * tok_dev * width,
        moved_bytes=4e6,
    )(tokens, row, norm_gain)

    def exchanged(value):
        flat = value.reshape((devices,) + message[2:])
        return lax.all_to_all(flat, AXES, split_axis=0, concat_axis=0, tiled=True).reshape(message)

    arrived = exchanged(sent)

    gate, places = call(
        functools.partial(side_kernel, capacity),
        [like((tok_dev, 1), F32), like((tok_dev, 2), jnp.int32)],
        [vmem()] * 4,
        flops=12 * tok_dev * experts * width,
        moved_bytes=4e6,
    )(tokens, row, norm_gain, router_weight)

    side = like((3 * FAR * size, width), BF16)
    own, right, left, up, down, far_scales = call(
        functools.partial(relay_kernel, size),
        [like((4 * FAR * size, width), BF16)] + [side] * 4 + [like((FAR, 1, shard), F32)],
        [vmem()] * FAR,
        [dma((16 * FAR,))],
        moved_bytes=6e6,
    )(*far)
    near = []
    for value, shift in ((right, {"dx": 1}), (left, {"dx": -1}), (up, {"dy": 1}), (down, {"dy": -1})):
        near.append(moved(value, nodes, **shift))
    pieces = [own] + near
    swapped = []
    for value in pieces:
        swapped.append(moved(value, nodes, dc=1))

    rows = devices * capacity
    produced = call(
        expert_kernel,
        like(message, BF16),
        [vmem(), hbm(), hbm()],
        [
            pltpu.VMEM((rows, width), BF16),
            pltpu.VMEM((rows, units), BF16),
            pltpu.VMEM((held_experts, width, units), BF16),
            pltpu.VMEM((held_experts, units, width), BF16),
            dma((8 * held_experts,)),
        ],
        grant=56,
        flops=4 * held_experts * rows * units * width,
        moved_bytes=2e7,
    )(arrived, expert_in, expert_out)
    returned = exchanged(produced)

    return call(
        functools.partial(tail_kernel, size),
        like(tokens.shape, BF16),
        [vmem()] * 8 + [hbm()] * 12,
        [
            pltpu.VMEM((units, width), BF16),
            pltpu.VMEM((units, width), BF16),
            pltpu.VMEM((tok_dev, width), BF16),
            pltpu.VMEM((tok_dev, width), BF16),
            pltpu.VMEM((tok_dev, units), BF16),
            pltpu.VMEM((tok_dev, width), F32),
            dma((2, FAR + 1)),
        ],
        grant=58,
        flops=4 * tok_dev * units * width,
        moved_bytes=1.2e7,
    )(
        tokens,
        gate,
        places,
        post_gain,
        scale_in,
        scale_out,
        far_scales,
        returned,
        dense_in,
        dense_out,
        *pieces,
        *swapped,
    )


def solution(mesh):
    return jax.shard_map(
        per_device,
        mesh=mesh,
        in_specs=(
            P(("node", "wide"), None),
            P(("node", "wide"), None),
            P(),
            P(),
            P(("node", "wide"), None, None),
            P(("node", "wide"), None, None),
            P(),
            P("node", None),
            P("node"),
            P("node", None),
            P(),
        ),
        out_specs=P(("node", "wide"), None),
        check_vma=False,
    )
```

```python
import functools

import jax
import jax.numpy as jnp
from jax import lax
from jax.experimental import pallas as pl
from jax.experimental.pallas import tpu as pltpu
from jax.sharding import PartitionSpec as P

AXES = ("node", "wide")
Y_CHIPS, X_CHIPS, CORES = 4, 4, 2
COLORS = 4
FAR = 3
SCALE_ROWS = 8
LANES = 128
SUB = 8
BF16 = jnp.bfloat16
F32 = jnp.float32


def moved(value, nodes, dz=0, dy=0, dx=0, dc=0):
    def place(z, y, x, c):
        return ((z * Y_CHIPS + y) * X_CHIPS + x) * CORES + c

    pairs = [
        (
            place(z, y, x, c),
            place((z + dz) % nodes, (y + dy) % Y_CHIPS, (x + dx) % X_CHIPS, (c + dc) % CORES),
        )
        for z in range(nodes)
        for y in range(Y_CHIPS)
        for x in range(X_CHIPS)
        for c in range(CORES)
    ]
    return lax.ppermute(value, AXES, pairs)


def position():
    wide = lax.axis_index("wide")
    core = wide % CORES
    x_chip = (wide // CORES) % X_CHIPS
    y_chip = wide // (CORES * X_CHIPS)
    return core, ((x_chip + 2 * y_chip) % COLORS, (2 * x_chip + y_chip) % COLORS)


def joined(first, second):
    top = lax.broadcasted_iota(jnp.int32, first.shape, 1) < SUB // 2
    even = jnp.where(top, first, pltpu.roll(second, SUB // 2, 1))
    odd = jnp.where(top, pltpu.roll(first, SUB // 2, 1), second)
    return even, odd


def pack_columns(rows, block, out_ref):
    count = rows.shape[0] // SUB
    first = rows[:, :LANES].reshape(count, SUB, LANES)
    second = rows[:, LANES:].reshape(count, SUB, LANES)
    even, odd = joined(first, second)
    out_ref[:, 0, block * SUB : (block + 1) * SUB, :] = even.astype(out_ref.dtype)
    out_ref[:, 1, block * SUB : (block + 1) * SUB, :] = odd.astype(out_ref.dtype)


def unpack_messages(message_ref, held, rows_ref):
    count = message_ref.shape[0]
    blocks = rows_ref.shape[1] // (2 * LANES)
    for block in range(blocks):
        tile = pl.ds(pl.multiple_of((held * blocks + block) * SUB, SUB), SUB)
        even = message_ref[:, 0, tile, :].astype(F32)
        odd = message_ref[:, 1, tile, :].astype(F32)
        first, second = joined(even, odd)
        start = block * 2 * LANES
        rows_ref[:, start : start + LANES] = first.reshape(count * SUB, LANES).astype(BF16)
        rows_ref[:, start + LANES : start + 2 * LANES] = second.reshape(count * SUB, LANES).astype(BF16)


def half_copy(source, target, held, held_experts, sems):
    tiles = source.shape[2] // held_experts
    part = pl.ds(held * tiles, tiles)
    return pltpu.make_async_copy(source.at[:, :, part, :], target.at[:, :, part, :], sems.at[held])


def both_ways(row):
    count = row.shape[1]
    floats = row.astype(F32)
    turned = jnp.broadcast_to(floats, (LANES, count)).T
    along_rows = jnp.concatenate([turned] * (count // LANES), axis=1)
    return jnp.broadcast_to(floats, (count, count)), along_rows


def normed_rows(floats, gain):
    square_mean = jnp.mean(floats * floats, axis=-1, keepdims=True)
    return (floats * lax.rsqrt(square_mean + 1e-06) * gain).astype(BF16)


def scale_terms(scale):
    high = scale.astype(BF16).astype(F32)
    middle = (scale - high).astype(BF16).astype(F32)
    low = scale - high - middle
    lines = lax.broadcasted_iota(jnp.int32, (SCALE_ROWS, scale.shape[1]), 0)
    terms = jnp.where(lines == 0, high, jnp.where(lines == 1, middle, jnp.where(lines == 2, low, 0.0)))
    return terms.astype(BF16)


def relay_kernel(size, *refs):
    far, (own, right, left, up, down, scales_ref) = refs[:FAR], refs[FAR:]
    for index, source in enumerate(far):
        for part in range(2):
            whole, shared = ((right, left), (up, down))[part], ((up, down), (right, left))[part]
            for which in range(2):
                start = (part * 2 + which) * size
                piece = source[start : start + size, :]
                for out, line in (
                    (own, (index * 2 + part) * 2 + which),
                    (whole[0], index * 2 + which),
                    (whole[1], index * 2 + which),
                    (shared[which], 2 * FAR + index),
                ):
                    out[line * size : (line + 1) * size, :] = piece
        terms = source[4 * size :, :].astype(F32)
        scales_ref[index] = terms[0:1] + terms[1:2] + terms[2:3]


def weave_copies(size, own_in, own_out, arrays, w_in, w_out, sems):
    shard = own_in.shape[0]
    core, colors = position()
    weights = (w_in, w_out)
    copies = [[[] for _ in range(FAR + 1)] for _ in range(2)]
    for which, own in enumerate((own_in, own_out)):
        copies[which][0].append(
            pltpu.make_async_copy(own, weights[which].at[pl.ds(0, shard), :], sems.at[which, 0])
        )

    def copy(array, row, index, part, which, color, swapped):
        line = (colors[part] + color) % COLORS
        line = line * CORES + (core + swapped) % CORES
        start = pl.multiple_of(shard * (index + 1) + part * (shard // 2) + line * size, 16)
        copies[which][index + 1].append(
            pltpu.make_async_copy(
                arrays[array].at[pl.ds(row * size, size), :],
                weights[which].at[pl.ds(start, size), :],
                sems.at[which, index + 1],
            )
        )

    for swapped in range(CORES):
        base = swapped * 5
        for index in range(FAR):
            for which in range(2):
                for part in range(2):
                    copy(base, (index * 2 + part) * 2 + which, index, part, which, 0, swapped)
                for side in range(4):
                    part, color = side // 2, (-1, 1)[side % 2]
                    copy(base + 1 + side, index * 2 + which, index, part, which, color, swapped)
                    if which == side % 2:
                        copy(base + 1 + side, 2 * FAR + index, index, 1 - part, which, 2, swapped)
    return copies


def cut_kernel(size, scale_hbm, in_hbm, out_hbm, cut_ref, scale_ref, sems, scale_sem):
    half = in_hbm.shape[0] // 2
    core, colors = position()
    copies = []
    for part in range(2):
        start = pl.multiple_of(part * half + (colors[part] * CORES + core) * size, 16)
        for which, codes in enumerate((in_hbm, out_hbm)):
            index = part * 2 + which
            held = cut_ref.at[pl.ds(index * size, size), :]
            copies.append(pltpu.make_async_copy(codes.at[pl.ds(start, size), :], held, sems.at[index]))
    scale_copy = pltpu.make_async_copy(scale_hbm, scale_ref, scale_sem.at[0])
    scale_copy.start()
    for copy in copies:
        copy.start()
    scale_copy.wait()
    cut_ref[4 * size :, :] = scale_terms(scale_ref[...].reshape(1, -1))
    for copy in copies:
        copy.wait()


def dispatch_kernel(capacity, token_ref, row_ref, gain_ref, out_hbm, out_ref, sems):
    normed = normed_rows(token_ref[...].astype(F32), gain_ref[...].reshape(1, -1))
    count = token_ref.shape[0]
    row = row_ref[...]
    along, across = both_ways(row)
    source = lax.broadcasted_iota(jnp.int32, (count, count), 0)
    target = lax.broadcasted_iota(jnp.int32, (count, count), 1)
    same = jnp.where((along == across) & (source < target), 1.0, 0.0)
    slot = jnp.sum(same, axis=0, keepdims=True).astype(jnp.int32)
    place = (row >> 1) * capacity + slot
    blocks = normed.shape[1] // (2 * LANES)
    copies = []
    for held in range(2):
        wanted = jnp.where((row & 1) == held, place, -1)
        selected = jnp.where(source == wanted, 1.0, 0.0).astype(BF16)
        for block in range(blocks):
            columns = normed[:, block * 2 * LANES : (block + 1) * 2 * LANES]
            rows = jnp.dot(selected, columns, preferred_element_type=F32)
            pack_columns(rows, held * blocks + block, out_ref)
        copies.append(half_copy(out_ref, out_hbm, held, 2, sems))
        copies[-1].start()
    for copy in copies:
        copy.wait()


def side_kernel(capacity, token_ref, row_ref, gain_ref, router_ref, marks_ref):
    normed = normed_rows(token_ref[...].astype(F32), gain_ref[...].reshape(1, -1)).astype(F32)
    count = token_ref.shape[0]
    along, across = both_ways(row_ref[...])
    logits = jnp.dot(normed, router_ref[...], precision=lax.Precision.HIGHEST, preferred_element_type=F32)
    experts = logits.shape[1]
    columns = lax.broadcasted_iota(jnp.int32, (count, experts), 1).astype(F32)
    picked = jnp.sum(jnp.where(across[:, :experts] == columns, logits, 0.0), axis=1, keepdims=True)
    gate = 1.0 / (1.0 + jnp.exp(-picked))
    rank = lax.broadcasted_iota(jnp.int32, (count, count), 0)
    other = lax.broadcasted_iota(jnp.int32, (count, count), 1)
    same = jnp.where((along == across) & (other < rank), 1.0, 0.0)
    slot = jnp.sum(same, axis=1, keepdims=True).astype(jnp.int32)
    chosen = across[:, :1].astype(jnp.int32)
    place = (chosen >> 1) * capacity + slot
    marks_ref[:, 0:1] = place.astype(F32)
    marks_ref[:, 1:2] = (chosen & 1).astype(F32)
    marks_ref[:, 2:3] = gate


def expert_kernel(
    message,
    in_hbm,
    out_hbm,
    result_hbm,
    result,
    rows,
    hidden,
    w_in,
    w_out,
    first_sems,
    in_sems,
    out_sems,
    result_sems,
):
    held_experts, width, units = in_hbm.shape
    tile, depth = 1024, 2
    steps, blocks = units // tile, width // (2 * LANES)

    def first_copy(step):
        columns = pl.ds(pl.multiple_of(step * tile, tile), tile)
        return pltpu.make_async_copy(
            in_hbm.at[0, :, columns], w_in.at[0, :, columns], first_sems.at[step]
        )

    def in_copy(held):
        return pltpu.make_async_copy(in_hbm.at[held], w_in.at[held], in_sems.at[held])

    def out_copy(held):
        return pltpu.make_async_copy(out_hbm.at[held], w_out.at[held], out_sems.at[held])

    def result_copy(held, block):
        part = pl.ds((held * blocks + block) * SUB, SUB)
        return pltpu.make_async_copy(
            result.at[:, :, part, :], result_hbm.at[:, :, part, :], result_sems.at[held * blocks + block]
        )

    for step in range(depth):
        first_copy(step).start()
    for held in range(held_experts):
        if held == 0:
            unpack_messages(message, held, rows.at[0])

        def enter(step, carry, held=held):
            if held == 0:
                first_copy(step).wait()

                @pl.when(step + depth < steps)
                def _():
                    first_copy(step + depth).start()

                @pl.when(step + depth == steps)
                def _():
                    out_copy(0).start()

            columns = pl.ds(pl.multiple_of(step * tile, tile), tile)
            value = jnp.dot(rows[held], w_in[held, :, columns], preferred_element_type=F32)
            hidden[:, columns] = jnp.maximum(value, 0.0).astype(BF16)
            return carry

        if held > 0:
            in_copy(held).wait()
            out_copy(held).start()
        lax.fori_loop(0, steps, enter, 0)
        out_copy(held).wait()
        if held + 1 < held_experts:
            in_copy(held + 1).start()
            unpack_messages(message, held + 1, rows.at[held + 1])
        for block in range(blocks):
            columns = slice(block * 2 * LANES, (block + 1) * 2 * LANES)
            value = jnp.dot(hidden[...], w_out[held, :, columns], preferred_element_type=F32)
            pack_columns(value, held * blocks + block, result)
            result_copy(held, block).start()
    for held in range(held_experts):
        for block in range(blocks):
            result_copy(held, block).wait()


def tail_kernel(
    size,
    gain_ref,
    scale_ref,
    scale_out_ref,
    far_scale_ref,
    tokens,
    message,
    marks_hbm,
    own_in,
    own_out,
    *refs,
):
    arrays = refs[:-13]
    result_hbm, result_ref, result_sems = refs[-13:-10]
    w_in, w_out, rows, normed2, hidden, total, scales, sems, marks, marks_sem = refs[-10:]
    copies = weave_copies(size, own_in, own_out, arrays, w_in, w_out, sems)
    held_experts = 2
    count, width = tokens.shape
    units = hidden.shape[1]
    shard = own_in.shape[0]
    marks_copy = pltpu.make_async_copy(marks_hbm, marks, marks_sem.at[0])
    marks_copy.start()
    for node in copies[0]:
        for copy in node:
            copy.start()
    total[...] = jnp.zeros_like(total)
    slots = lax.broadcasted_iota(jnp.int32, (count, count), 1).astype(F32)

    def combine(held, carry):
        unpack_messages(message, held, rows)

        @pl.when(held == 0)
        def _():
            marks_copy.wait()

        chosen = (slots == marks[:, 0:1]) & (marks[:, 1:2] == held.astype(F32))
        picked = jnp.where(chosen, 1.0, 0.0).astype(BF16)
        total[...] += jnp.dot(picked, rows[...], preferred_element_type=F32)
        return carry

    lax.fori_loop(0, held_experts, combine, 0)
    residual = (tokens[...].astype(F32) + marks[:, 2:3] * total[...]).astype(BF16)
    rows[...] = residual
    normed2[...] = normed_rows(residual.astype(F32), gain_ref[...].reshape(1, -1))

    scales[:, :shard] = scale_ref[...].reshape(1, -1)
    for index in range(FAR):
        scales[:, (index + 1) * shard : (index + 2) * shard] = far_scale_ref[index]

    def enter(step, carry):
        columns = pl.ds(pl.multiple_of(step * tile, tile), tile)
        value = lax.dot_general(
            normed2[...],
            w_in[columns, :],
            (((1,), (1,)), ((), ())),
            preferred_element_type=F32,
        )
        hidden[:, columns] = jnp.maximum(value * scales[:, columns], 0.0).astype(BF16)
        return carry

    tile = 1024
    bounds = (0, 1, units // tile)
    for part in range(2):
        for node in copies[0][part * (FAR + 1) // 2 : (part + 1) * (FAR + 1) // 2]:
            for copy in node:
                copy.wait()
        if part == 0:
            for node in copies[1]:
                for copy in node:
                    copy.start()
        lax.fori_loop(bounds[part], bounds[part + 1], enter, 0)
    for node in copies[1]:
        for copy in node:
            copy.wait()
    scale_out = scale_out_ref[...].reshape(1, -1)
    tile = 256
    results = []
    for step in range(width // tile):
        columns = slice(step * tile, (step + 1) * tile)
        value = jnp.dot(hidden[...], w_out[:, columns], preferred_element_type=F32)
        value = rows[:, columns].astype(F32) + value * scale_out[:, columns]
        result_ref[:, columns] = value.astype(BF16)
        results.append(
            pltpu.make_async_copy(
                result_ref.at[:, columns], result_hbm.at[:, columns], result_sems.at[step]
            )
        )
        results[-1].start()
    for copy in results:
        copy.wait()


def vmem():
    return pl.BlockSpec(memory_space=pltpu.VMEM)


def hbm():
    return pl.BlockSpec(memory_space=pltpu.HBM)


def call(kernel, out_shape, in_specs, scratch=(), grant=16, out_spec=None, flops=0, moved_bytes=0):
    return pl.pallas_call(
        kernel,
        out_shape=out_shape,
        in_specs=in_specs,
        out_specs=jax.tree.map(lambda _: out_spec or vmem(), out_shape),
        scratch_shapes=list(scratch),
        compiler_params=pltpu.CompilerParams(vmem_limit_bytes=grant << 20),
        cost_estimate=pl.CostEstimate(
            flops=int(flops), bytes_accessed=int(moved_bytes), transcendentals=0
        ),
    )


def stay(value):
    return pltpu.with_memory_space_constraint(value, pltpu.HBM)


def per_device(
    tokens,
    expert_index,
    norm_gain,
    router_weight,
    expert_in,
    expert_out,
    post_gain,
    dense_in,
    scale_in,
    dense_out,
    scale_out,
):
    tok_dev, width = tokens.shape
    experts = router_weight.shape[1]
    held_experts, _, units = expert_in.shape
    devices = experts // held_experts
    capacity = max(2, 2 * tok_dev // experts)
    shard = dense_in.shape[0]
    nodes = units // shard
    size = shard // 2 // (COLORS * CORES)
    message = (devices // 2, 2, held_experts * capacity * width // LANES, LANES)
    like = jax.ShapeDtypeStruct

    row = expert_index.reshape(1, tok_dev)
    dma = pltpu.SemaphoreType.DMA

    cut = call(
        functools.partial(cut_kernel, size),
        like((4 * size + SCALE_ROWS, width), BF16),
        [hbm()] * 3,
        [pltpu.VMEM((shard,), F32), dma((4,)), dma((1,))],
        grant=16,
        moved_bytes=6e5,
    )(stay(scale_in), stay(dense_in), stay(dense_out))
    sent = call(
        functools.partial(dispatch_kernel, capacity),
        like(message, BF16),
        [vmem()] * 3,
        [pltpu.VMEM(message, BF16), dma((held_experts,))],
        out_spec=hbm(),
        flops=4 * tok_dev * tok_dev * width,
        moved_bytes=4e6,
    )(tokens, row, norm_gain)

    far = []
    for step in (1, -1, 2):
        far.append(moved(cut, nodes, dz=step))

    def exchanged(value):
        flat = value.reshape((devices,) + message[2:])
        return lax.all_to_all(flat, AXES, split_axis=0, concat_axis=0, tiled=True).reshape(message)

    arrived = exchanged(sent)

    marks = call(
        functools.partial(side_kernel, capacity),
        like((tok_dev, 3), F32),
        [vmem()] * 4,
        flops=12 * tok_dev * experts * width,
        moved_bytes=4e6,
    )(tokens, row, norm_gain, router_weight)

    side = like((3 * FAR * size, width), BF16)
    own, right, left, up, down, far_scales = call(
        functools.partial(relay_kernel, size),
        [like((4 * FAR * size, width), BF16)] + [side] * 4 + [like((FAR, 1, shard), F32)],
        [vmem()] * FAR,
        moved_bytes=6e6,
    )(*far)
    near = []
    for value, shift in ((right, {"dx": 1}), (left, {"dx": -1}), (up, {"dy": 1}), (down, {"dy": -1})):
        near.append(moved(value, nodes, **shift))
    pieces = [own] + near
    swapped = []
    for value in pieces:
        swapped.append(moved(value, nodes, dc=1))

    rows = devices * capacity
    produced = call(
        expert_kernel,
        like(message, BF16),
        [vmem()] + [hbm()] * 2,
        [
            pltpu.VMEM(message, BF16),
            pltpu.VMEM((held_experts, rows, width), BF16),
            pltpu.VMEM((rows, units), BF16),
            pltpu.VMEM((held_experts, width, units), BF16),
            pltpu.VMEM((held_experts, units, width), BF16),
            dma((units // 1024,)),
            dma((held_experts,)),
            dma((held_experts,)),
            dma((held_experts * width // (2 * LANES),)),
        ],
        grant=40,
        out_spec=hbm(),
        flops=4 * held_experts * rows * units * width,
        moved_bytes=2e7,
    )(arrived, stay(expert_in), stay(expert_out))
    returned = exchanged(produced)

    return call(
        functools.partial(tail_kernel, size),
        like(tokens.shape, BF16),
        [vmem()] * 6 + [hbm()] * 13,
        [
            pltpu.VMEM((tok_dev, width), BF16),
            dma((width // 256,)),
            pltpu.VMEM((units, width), BF16),
            pltpu.VMEM((units, width), BF16),
            pltpu.VMEM((tok_dev, width), BF16),
            pltpu.VMEM((tok_dev, width), BF16),
            pltpu.VMEM((tok_dev, units), BF16),
            pltpu.VMEM((tok_dev, width), F32),
            pltpu.VMEM((1, units), F32),
            dma((2, FAR + 1)),
            pltpu.VMEM((tok_dev, 3), F32),
            dma((1,)),
        ],
        grant=40,
        out_spec=hbm(),
        flops=4 * tok_dev * units * width,
        moved_bytes=1.2e7,
    )(
        post_gain,
        scale_in,
        scale_out,
        far_scales,
        tokens,
        returned,
        *map(stay, [marks, dense_in, dense_out] + pieces + swapped),
    )


def solution(mesh):
    return jax.shard_map(
        per_device,
        mesh=mesh,
        in_specs=(
            P(("node", "wide"), None),
            P(("node", "wide"), None),
            P(),
            P(),
            P(("node", "wide"), None, None),
            P(("node", "wide"), None, None),
            P(),
            P("node", None),
            P("node"),
            P("node", None),
            P(),
        ),
        out_specs=P(("node", "wide"), None),
        check_vma=False,
    )
```

```python
import functools

import jax
import jax.numpy as jnp
from jax import lax
from jax.experimental import pallas as pl
from jax.experimental.pallas import tpu as pltpu
from jax.sharding import PartitionSpec as P

AXES = ("node", "wide")
Y_CHIPS, X_CHIPS, CORES = 4, 4, 2
COLORS = 4
FAR = 3
SCALE_ROWS = 8
LANES = 128
SUB = 8
BF16 = jnp.bfloat16
F32 = jnp.float32


def moved(value, nodes, dz=0, dy=0, dx=0, dc=0):
    def place(z, y, x, c):
        return ((z * Y_CHIPS + y) * X_CHIPS + x) * CORES + c

    pairs = [
        (
            place(z, y, x, c),
            place((z + dz) % nodes, (y + dy) % Y_CHIPS, (x + dx) % X_CHIPS, (c + dc) % CORES),
        )
        for z in range(nodes)
        for y in range(Y_CHIPS)
        for x in range(X_CHIPS)
        for c in range(CORES)
    ]
    return lax.ppermute(value, AXES, pairs)


def position():
    wide = lax.axis_index("wide")
    core = wide % CORES
    x_chip = (wide // CORES) % X_CHIPS
    y_chip = wide // (CORES * X_CHIPS)
    return core, ((x_chip + 2 * y_chip) % COLORS, (2 * x_chip + y_chip) % COLORS)


def joined(first, second):
    top = lax.broadcasted_iota(jnp.int32, first.shape, 1) < SUB // 2
    even = jnp.where(top, first, pltpu.roll(second, SUB // 2, 1))
    odd = jnp.where(top, pltpu.roll(first, SUB // 2, 1), second)
    return even, odd


def pack_columns(rows, block, out_ref):
    count = rows.shape[0] // SUB
    first = rows[:, :LANES].reshape(count, SUB, LANES)
    second = rows[:, LANES:].reshape(count, SUB, LANES)
    even, odd = joined(first, second)
    out_ref[:, 0, block * SUB : (block + 1) * SUB, :] = even.astype(out_ref.dtype)
    out_ref[:, 1, block * SUB : (block + 1) * SUB, :] = odd.astype(out_ref.dtype)


def unpack_messages(message_ref, held, rows_ref):
    count = message_ref.shape[0]
    blocks = rows_ref.shape[1] // (2 * LANES)
    for block in range(blocks):
        tile = pl.ds(pl.multiple_of((held * blocks + block) * SUB, SUB), SUB)
        even = message_ref[:, 0, tile, :].astype(F32)
        odd = message_ref[:, 1, tile, :].astype(F32)
        first, second = joined(even, odd)
        start = block * 2 * LANES
        rows_ref[:, start : start + LANES] = first.reshape(count * SUB, LANES).astype(BF16)
        rows_ref[:, start + LANES : start + 2 * LANES] = second.reshape(count * SUB, LANES).astype(BF16)


def half_copy(source, target, held, held_experts, sems):
    tiles = source.shape[2] // held_experts
    part = pl.ds(held * tiles, tiles)
    return pltpu.make_async_copy(source.at[:, :, part, :], target.at[:, :, part, :], sems.at[held])


def both_ways(row):
    count = row.shape[1]
    floats = row.astype(F32)
    turned = jnp.broadcast_to(floats, (LANES, count)).T
    along_rows = jnp.concatenate([turned] * (count // LANES), axis=1)
    return jnp.broadcast_to(floats, (count, count)), along_rows


def normed_rows(floats, gain):
    square_mean = jnp.mean(floats * floats, axis=-1, keepdims=True)
    return (floats * lax.rsqrt(square_mean + 1e-06) * gain).astype(BF16)


def scale_terms(scale):
    high = scale.astype(BF16).astype(F32)
    middle = (scale - high).astype(BF16).astype(F32)
    low = scale - high - middle
    lines = lax.broadcasted_iota(jnp.int32, (SCALE_ROWS, scale.shape[1]), 0)
    terms = jnp.where(lines == 0, high, jnp.where(lines == 1, middle, jnp.where(lines == 2, low, 0.0)))
    return terms.astype(BF16)


def relay_kernel(size, *refs):
    far, (own, right, left, up, down, scales_ref) = refs[:FAR], refs[FAR:]
    for index, source in enumerate(far):
        for part in range(2):
            whole, shared = ((right, left), (up, down))[part], ((up, down), (right, left))[part]
            for which in range(2):
                start = (part * 2 + which) * size
                piece = source[start : start + size, :]
                for out, line in (
                    (own, (index * 2 + part) * 2 + which),
                    (whole[0], index * 2 + which),
                    (whole[1], index * 2 + which),
                    (shared[which], 2 * FAR + index),
                ):
                    out[line * size : (line + 1) * size, :] = piece
        terms = source[4 * size :, :].astype(F32)
        scales_ref[index] = terms[0:1] + terms[1:2] + terms[2:3]


def weave_copies(size, own_in, own_out, arrays, w_in, w_out, sems):
    shard = own_in.shape[0]
    core, colors = position()
    weights = (w_in, w_out)
    copies = [[[] for _ in range(FAR + 1)] for _ in range(2)]
    for which, own in enumerate((own_in, own_out)):
        copies[which][0].append(
            pltpu.make_async_copy(own, weights[which].at[pl.ds(0, shard), :], sems.at[which, 0])
        )

    def copy(array, row, index, part, which, color, swapped):
        line = (colors[part] + color) % COLORS
        line = line * CORES + (core + swapped) % CORES
        start = pl.multiple_of(shard * (index + 1) + part * (shard // 2) + line * size, 16)
        copies[which][index + 1].append(
            pltpu.make_async_copy(
                arrays[array].at[pl.ds(row * size, size), :],
                weights[which].at[pl.ds(start, size), :],
                sems.at[which, index + 1],
            )
        )

    for swapped in range(CORES):
        base = swapped * 5
        for index in range(FAR):
            for which in range(2):
                for part in range(2):
                    copy(base, (index * 2 + part) * 2 + which, index, part, which, 0, swapped)
                for side in range(4):
                    part, color = side // 2, (-1, 1)[side % 2]
                    copy(base + 1 + side, index * 2 + which, index, part, which, color, swapped)
                    if which == side % 2:
                        copy(base + 1 + side, 2 * FAR + index, index, 1 - part, which, 2, swapped)
    return copies


def cut_kernel(size, scale_hbm, in_hbm, out_hbm, cut_ref, scale_ref, sems, scale_sem):
    half = in_hbm.shape[0] // 2
    core, colors = position()
    copies = []
    for part in range(2):
        start = pl.multiple_of(part * half + (colors[part] * CORES + core) * size, 16)
        for which, codes in enumerate((in_hbm, out_hbm)):
            index = part * 2 + which
            held = cut_ref.at[pl.ds(index * size, size), :]
            copies.append(pltpu.make_async_copy(codes.at[pl.ds(start, size), :], held, sems.at[index]))
    scale_copy = pltpu.make_async_copy(scale_hbm, scale_ref, scale_sem.at[0])
    scale_copy.start()
    for copy in copies:
        copy.start()
    scale_copy.wait()
    cut_ref[4 * size :, :] = scale_terms(scale_ref[...].reshape(1, -1))
    for copy in copies:
        copy.wait()


def dispatch_kernel(capacity, token_ref, row_ref, gain_ref, out_hbm, out_ref, sems):
    normed = normed_rows(token_ref[...].astype(F32), gain_ref[...].reshape(1, -1))
    count = token_ref.shape[0]
    row = row_ref[...]
    along, across = both_ways(row)
    source = lax.broadcasted_iota(jnp.int32, (count, count), 0)
    target = lax.broadcasted_iota(jnp.int32, (count, count), 1)
    same = jnp.where((along == across) & (source < target), 1.0, 0.0)
    slot = jnp.sum(same, axis=0, keepdims=True).astype(jnp.int32)
    place = (row >> 1) * capacity + slot
    blocks = normed.shape[1] // (2 * LANES)
    copies = []
    for held in range(2):
        wanted = jnp.where((row & 1) == held, place, -1)
        selected = jnp.where(source == wanted, 1.0, 0.0).astype(BF16)
        for block in range(blocks):
            columns = normed[:, block * 2 * LANES : (block + 1) * 2 * LANES]
            rows = jnp.dot(selected, columns, preferred_element_type=F32)
            pack_columns(rows, held * blocks + block, out_ref)
        copies.append(half_copy(out_ref, out_hbm, held, 2, sems))
        copies[-1].start()
    for copy in copies:
        copy.wait()


def side_kernel(capacity, token_ref, row_ref, gain_ref, router_ref, marks_ref):
    normed = normed_rows(token_ref[...].astype(F32), gain_ref[...].reshape(1, -1)).astype(F32)
    count = token_ref.shape[0]
    along, across = both_ways(row_ref[...])
    logits = jnp.dot(normed, router_ref[...], precision=lax.Precision.HIGHEST, preferred_element_type=F32)
    experts = logits.shape[1]
    columns = lax.broadcasted_iota(jnp.int32, (count, experts), 1).astype(F32)
    picked = jnp.sum(jnp.where(across[:, :experts] == columns, logits, 0.0), axis=1, keepdims=True)
    gate = 1.0 / (1.0 + jnp.exp(-picked))
    rank = lax.broadcasted_iota(jnp.int32, (count, count), 0)
    other = lax.broadcasted_iota(jnp.int32, (count, count), 1)
    same = jnp.where((along == across) & (other < rank), 1.0, 0.0)
    slot = jnp.sum(same, axis=1, keepdims=True).astype(jnp.int32)
    chosen = across[:, :1].astype(jnp.int32)
    place = (chosen >> 1) * capacity + slot
    marks_ref[:, 0:1] = place.astype(F32)
    marks_ref[:, 1:2] = (chosen & 1).astype(F32)
    marks_ref[:, 2:3] = gate


def expert_kernel(
    message,
    in_hbm,
    out_hbm,
    result_hbm,
    result,
    rows,
    hidden,
    w_in,
    w_out,
    first_sems,
    in_sems,
    out_sems,
    result_sems,
):
    held_experts, width, units = in_hbm.shape
    tile, depth = 1024, 2
    steps, blocks = units // tile, width // (2 * LANES)

    def first_copy(step):
        columns = pl.ds(pl.multiple_of(step * tile, tile), tile)
        return pltpu.make_async_copy(
            in_hbm.at[0, :, columns], w_in.at[0, :, columns], first_sems.at[step]
        )

    def half_tile_copy(half):
        columns = pl.ds(pl.multiple_of(half * (tile // 2), tile // 2), tile // 2)
        return pltpu.make_async_copy(
            in_hbm.at[0, :, columns], w_in.at[0, :, columns], first_sems.at[half * steps]
        )

    def in_copy(held):
        return pltpu.make_async_copy(in_hbm.at[held], w_in.at[held], in_sems.at[held])

    def out_copy(held):
        return pltpu.make_async_copy(out_hbm.at[held], w_out.at[held], out_sems.at[held])

    def result_copy(held, block):
        part = pl.ds((held * blocks + block) * SUB, SUB)
        return pltpu.make_async_copy(
            result.at[:, :, part, :], result_hbm.at[:, :, part, :], result_sems.at[held * blocks + block]
        )

    for half in range(2):
        half_tile_copy(half).start()
    for step in range(1, depth):
        first_copy(step).start()
    for held in range(held_experts):
        if held == 0:
            unpack_messages(message, held, rows.at[0])

        def enter(step, carry, held=held):
            if held == 0:
                first_copy(step).wait()

                @pl.when(step + depth < steps)
                def _():
                    first_copy(step + depth).start()

                @pl.when(step + depth == steps)
                def _():
                    out_copy(0).start()

            columns = pl.ds(pl.multiple_of(step * tile, tile), tile)
            value = jnp.dot(rows[held], w_in[held, :, columns], preferred_element_type=F32)
            hidden[:, columns] = jnp.maximum(value, 0.0).astype(BF16)
            return carry

        def enter_half(half, carry):
            half_tile_copy(half).wait()

            @pl.when(half == 0)
            def _():
                first_copy(depth).start()

            columns = pl.ds(pl.multiple_of(half * (tile // 2), tile // 2), tile // 2)
            value = jnp.dot(rows[0], w_in[0, :, columns], preferred_element_type=F32)
            hidden[:, columns] = jnp.maximum(value, 0.0).astype(BF16)
            return carry

        if held > 0:
            in_copy(held).wait()
            out_copy(held).start()
            lax.fori_loop(0, steps, enter, 0)
        else:
            lax.fori_loop(0, 2, enter_half, 0)
            lax.fori_loop(1, steps, enter, 0)
        out_copy(held).wait()
        if held + 1 < held_experts:
            in_copy(held + 1).start()
            unpack_messages(message, held + 1, rows.at[held + 1])
        for block in range(blocks):
            columns = slice(block * 2 * LANES, (block + 1) * 2 * LANES)
            value = jnp.dot(hidden[...], w_out[held, :, columns], preferred_element_type=F32)
            pack_columns(value, held * blocks + block, result)
            result_copy(held, block).start()
    for held in range(held_experts):
        for block in range(blocks):
            result_copy(held, block).wait()


def tail_kernel(
    size,
    gain_ref,
    scale_ref,
    scale_out_ref,
    far_scale_ref,
    tokens,
    message,
    marks_hbm,
    own_in,
    own_out,
    *refs,
):
    arrays = refs[:-13]
    result_hbm, result_ref, result_sems = refs[-13:-10]
    w_in, w_out, rows, normed2, hidden, total, scales, sems, marks, marks_sem = refs[-10:]
    copies = weave_copies(size, own_in, own_out, arrays, w_in, w_out, sems)
    held_experts = 2
    count, width = tokens.shape
    units = hidden.shape[1]
    shard = own_in.shape[0]
    marks_copy = pltpu.make_async_copy(marks_hbm, marks, marks_sem.at[0])
    marks_copy.start()
    for node in copies[0]:
        for copy in node:
            copy.start()
    total[...] = jnp.zeros_like(total)
    slots = lax.broadcasted_iota(jnp.int32, (count, count), 1).astype(F32)

    def combine(held, carry):
        unpack_messages(message, held, rows)

        @pl.when(held == 0)
        def _():
            marks_copy.wait()

        chosen = (slots == marks[:, 0:1]) & (marks[:, 1:2] == held.astype(F32))
        picked = jnp.where(chosen, 1.0, 0.0).astype(BF16)
        total[...] += jnp.dot(picked, rows[...], preferred_element_type=F32)
        return carry

    lax.fori_loop(0, held_experts, combine, 0)
    residual = (tokens[...].astype(F32) + marks[:, 2:3] * total[...]).astype(BF16)
    rows[...] = residual
    normed2[...] = normed_rows(residual.astype(F32), gain_ref[...].reshape(1, -1))

    scales[:, :shard] = scale_ref[...].reshape(1, -1)
    for index in range(FAR):
        scales[:, (index + 1) * shard : (index + 2) * shard] = far_scale_ref[index]

    def enter(step, carry):
        columns = pl.ds(pl.multiple_of(step * tile, tile), tile)
        value = lax.dot_general(
            normed2[...],
            w_in[columns, :],
            (((1,), (1,)), ((), ())),
            preferred_element_type=F32,
        )
        hidden[:, columns] = jnp.maximum(value * scales[:, columns], 0.0).astype(BF16)
        return carry

    tile = 1024
    bounds = (0, 1, units // tile)
    for part in range(2):
        for node in copies[0][part * (FAR + 1) // 2 : (part + 1) * (FAR + 1) // 2]:
            for copy in node:
                copy.wait()
        if part == 0:
            for node in copies[1]:
                for copy in node:
                    copy.start()
        lax.fori_loop(bounds[part], bounds[part + 1], enter, 0)
    for node in copies[1]:
        for copy in node:
            copy.wait()
    scale_out = scale_out_ref[...].reshape(1, -1)
    tile = 256
    results = []
    for step in range(width // tile):
        columns = slice(step * tile, (step + 1) * tile)
        value = jnp.dot(hidden[...], w_out[:, columns], preferred_element_type=F32)
        value = rows[:, columns].astype(F32) + value * scale_out[:, columns]
        result_ref[:, columns] = value.astype(BF16)
        results.append(
            pltpu.make_async_copy(
                result_ref.at[:, columns], result_hbm.at[:, columns], result_sems.at[step]
            )
        )
        results[-1].start()
    for copy in results:
        copy.wait()


def vmem():
    return pl.BlockSpec(memory_space=pltpu.VMEM)


def hbm():
    return pl.BlockSpec(memory_space=pltpu.HBM)


def call(kernel, out_shape, in_specs, scratch=(), grant=16, out_spec=None, flops=0, moved_bytes=0):
    return pl.pallas_call(
        kernel,
        out_shape=out_shape,
        in_specs=in_specs,
        out_specs=jax.tree.map(lambda _: out_spec or vmem(), out_shape),
        scratch_shapes=list(scratch),
        compiler_params=pltpu.CompilerParams(vmem_limit_bytes=grant << 20),
        cost_estimate=pl.CostEstimate(
            flops=int(flops), bytes_accessed=int(moved_bytes), transcendentals=0
        ),
    )


def stay(value):
    return pltpu.with_memory_space_constraint(value, pltpu.HBM)


def per_device(
    tokens,
    expert_index,
    norm_gain,
    router_weight,
    expert_in,
    expert_out,
    post_gain,
    dense_in,
    scale_in,
    dense_out,
    scale_out,
):
    tok_dev, width = tokens.shape
    experts = router_weight.shape[1]
    held_experts, _, units = expert_in.shape
    devices = experts // held_experts
    capacity = max(2, 2 * tok_dev // experts)
    shard = dense_in.shape[0]
    nodes = units // shard
    size = shard // 2 // (COLORS * CORES)
    message = (devices // 2, 2, held_experts * capacity * width // LANES, LANES)
    like = jax.ShapeDtypeStruct

    row = expert_index.reshape(1, tok_dev)
    dma = pltpu.SemaphoreType.DMA

    cut = call(
        functools.partial(cut_kernel, size),
        like((4 * size + SCALE_ROWS, width), BF16),
        [hbm()] * 3,
        [pltpu.VMEM((shard,), F32), dma((4,)), dma((1,))],
        grant=16,
        moved_bytes=6e5,
    )(stay(scale_in), stay(dense_in), stay(dense_out))
    sent = call(
        functools.partial(dispatch_kernel, capacity),
        like(message, BF16),
        [vmem()] * 3,
        [pltpu.VMEM(message, BF16), dma((held_experts,))],
        out_spec=hbm(),
        flops=4 * tok_dev * tok_dev * width,
        moved_bytes=4e6,
    )(tokens, row, norm_gain)

    far = []
    for step in (1, -1, 2):
        far.append(moved(cut, nodes, dz=step))

    def exchanged(value):
        flat = value.reshape((devices,) + message[2:])
        return lax.all_to_all(flat, AXES, split_axis=0, concat_axis=0, tiled=True).reshape(message)

    arrived = exchanged(sent)

    marks = call(
        functools.partial(side_kernel, capacity),
        like((tok_dev, 3), F32),
        [vmem()] * 4,
        flops=12 * tok_dev * experts * width,
        moved_bytes=4e6,
    )(tokens, row, norm_gain, router_weight)

    side = like((3 * FAR * size, width), BF16)
    own, right, left, up, down, far_scales = call(
        functools.partial(relay_kernel, size),
        [like((4 * FAR * size, width), BF16)] + [side] * 4 + [like((FAR, 1, shard), F32)],
        [vmem()] * FAR,
        moved_bytes=6e6,
    )(*far)
    near = []
    for value, shift in ((right, {"dx": 1}), (left, {"dx": -1}), (up, {"dy": 1}), (down, {"dy": -1})):
        near.append(moved(value, nodes, **shift))
    pieces = [own] + near
    swapped = []
    for value in pieces:
        swapped.append(moved(value, nodes, dc=1))

    rows = devices * capacity
    produced = call(
        expert_kernel,
        like(message, BF16),
        [vmem()] + [hbm()] * 2,
        [
            pltpu.VMEM(message, BF16),
            pltpu.VMEM((held_experts, rows, width), BF16),
            pltpu.VMEM((rows, units), BF16),
            pltpu.VMEM((held_experts, width, units), BF16),
            pltpu.VMEM((held_experts, units, width), BF16),
            dma((units // 1024 + 1,)),
            dma((held_experts,)),
            dma((held_experts,)),
            dma((held_experts * width // (2 * LANES),)),
        ],
        grant=40,
        out_spec=hbm(),
        flops=4 * held_experts * rows * units * width,
        moved_bytes=2e7,
    )(arrived, stay(expert_in), stay(expert_out))
    returned = exchanged(produced)

    return call(
        functools.partial(tail_kernel, size),
        like(tokens.shape, BF16),
        [vmem()] * 6 + [hbm()] * 13,
        [
            pltpu.VMEM((tok_dev, width), BF16),
            dma((width // 256,)),
            pltpu.VMEM((units, width), BF16),
            pltpu.VMEM((units, width), BF16),
            pltpu.VMEM((tok_dev, width), BF16),
            pltpu.VMEM((tok_dev, width), BF16),
            pltpu.VMEM((tok_dev, units), BF16),
            pltpu.VMEM((tok_dev, width), F32),
            pltpu.VMEM((1, units), F32),
            dma((2, FAR + 1)),
            pltpu.VMEM((tok_dev, 3), F32),
            dma((1,)),
        ],
        grant=40,
        out_spec=hbm(),
        flops=4 * tok_dev * units * width,
        moved_bytes=1.2e7,
    )(
        post_gain,
        scale_in,
        scale_out,
        far_scales,
        tokens,
        returned,
        *map(stay, [marks, dense_in, dense_out] + pieces + swapped),
    )


def solution(mesh):
    return jax.shard_map(
        per_device,
        mesh=mesh,
        in_specs=(
            P(("node", "wide"), None),
            P(("node", "wide"), None),
            P(),
            P(),
            P(("node", "wide"), None, None),
            P(("node", "wide"), None, None),
            P(),
            P("node", None),
            P("node"),
            P("node", None),
            P(),
        ),
        out_specs=P(("node", "wide"), None),
        check_vma=False,
    )
```
